128 devices in a mesh: irrep: 8 (over z, x_lo), row: 16 (over y, x_hi, core).
Axes of the slice: x: 4 (x_hi: 2, x_lo: 2; x = x_hi * 2 + x_lo), y: 4, z: 4, core: 2. Of those that a mesh axis runs over, the one named last changes fastest.
Arguments:
- densities: float32 [8, 4096, 512], P('irrep', 'row'), may hold values from -6 to 6
- reduced_kernel: float32 [8, 24576, 4096], P('irrep', 'row'), may hold values from -0.09375 to 0.09375
Outputs:
- potentials: float32 [8, 24576, 512], P('irrep', 'row')
The draws below stay inside these ranges and needn't reach their ends.
All inputs are finite; a program needn't handle non-finite values.
Results may differ from the reference program's by a relative error of at most 0.000086.
Values sent between devices are 32-bit elements; how exact they have to be, the bound alone decides.
A program may use at most 128 MiB of HBM per device.

```python
import math
import jax
import jax.numpy as jnp
from jax import lax

EXCITE = 512
TARGETS = 24576
SOURCES = 4096
N_IRREP = 8


def level_of(rng, dims, shards, least, top_value):
    loudness, own = 1.0, jax.random.fold_in(rng, 6)
    for axis_at, shards_of in shards:
        heights = jnp.exp(jax.random.uniform(jax.random.fold_in(own, axis_at), (shards_of,), jnp.float32, least / len(shards), top_value / len(shards)))
        loudness = loudness * jnp.repeat(heights, dims[axis_at] // shards_of).reshape([-1 if axis == axis_at else 1 for axis in range(len(dims))])
    return loudness


def noise(rng, shape, spread, bound, split=(), dtype=jnp.bfloat16):
    loudness = level_of(rng, shape, split, -0.22, 0.18) if split else 1.0
    values = jax.random.normal(rng, shape, jnp.float32) * spread * loudness
    return jnp.minimum(jnp.maximum(values, -bound), bound).astype(dtype)


def setup_inputs(seed: int = 0) -> dict:
    arg_keys = jax.random.split(jax.random.key(seed), 3)
    return {
        "densities": noise(arg_keys[0], (N_IRREP, SOURCES, EXCITE), 1.0, 6.0, ((0, 8), (1, 16)), jnp.float32),
        "reduced_kernel": noise(arg_keys[1], (N_IRREP, TARGETS, SOURCES), SOURCES ** -0.5, 0.09375, ((0, 8), (1, 16)), jnp.float32),
    }


def sign_table(count):
    rows_iota = lax.broadcasted_iota(jnp.int32, (count, count), 0)
    cols_iota = lax.broadcasted_iota(jnp.int32, (count, count), 1)
    parity = jnp.zeros((count, count), jnp.int32)
    for level in range(count.bit_length() - 1):
        parity = parity + (rows_iota >> level & 1) * (cols_iota >> level & 1)
    return (1 - 2 * (parity % 2)).astype(jnp.float32)

def apply_tile(operands):
    return jnp.dot(operands[0], operands[1], precision=lax.Precision.HIGHEST, preferred_element_type=jnp.float32)

def reference(densities, reduced_kernel):
    norm_scale = 1.0 / math.sqrt(N_IRREP)
    folded = jnp.einsum('cg,gse->cse', sign_table(N_IRREP), densities, precision=lax.Precision.HIGHEST) * norm_scale
    return lax.map(apply_tile, (reduced_kernel, folded))
```

```python
import math

import jax
import jax.numpy as jnp
from jax import lax
from jax.experimental import pallas as pl
from jax.experimental.pallas import tpu as pltpu
from jax.sharding import PartitionSpec as P

F32, BF16 = jnp.float32, jnp.bfloat16
MESH = pl.DeviceIdType.MESH
HALF = 256

SLOTS = ("00", "30", "10", "01", "20", "31", "11", "21")
SLOT = {name: i for i, name in enumerate(SLOTS)}

UNIT_ROWS = (64, 64, 64, 64)
PIECE = 128
FIRST_PRODUCT = 10.0
SPLIT_PRODUCT = True


def units_of(rows):
    units = []
    for q in range(2):
        start = 0
        for count in rows:
            units.append((q, start, count))
            start += count
    return units


def plan(units, piece, first_product, split):
    link_rate, core_rate = 94e3, 440e3
    hop, two_hops, on_chip = 1.6, 2.4, 0.9
    steps, copies = {}, {}

    def cover(q, start, count):
        return [u for u, (uq, a, n) in enumerate(units) if uq == q and a < start + count and start < a + n]

    pieces = [(q, start) for q in range(2) for start in range(0, HALF, piece)]
    for u, (q, start, count) in enumerate(units):
        for flow in ("L1", "L2", "L3", "yp", "ym", "x2"):
            link = {"L1": "xi", "L2": "zA", "L3": "zB"}.get(flow, flow)
            copies[(flow, u)] = (link, count * HALF * 4)
        steps[("A1", u)] = (0, [("L1", u)], [], 0.1, [("L2", u)])
        steps[("A2", u)] = (0, [("L2", u)], [("A1", u)], 0.1, [("L3", u)])
        steps[("A3", u)] = (0, [("L3", u)], [("A2", u)], 0.1, [("x2", u), ("yp", u), ("ym", u)])
    for q, start in pieces:
        parts = cover(q, start, piece)
        size = piece * HALF * 4
        source = ("ym", "yp")[q]
        copies[("F", q, start)] = (source, size)
        steps[("FW", q, start)] = (1, [(source, u) for u in parts], [], 0.05, [("F", q, start)])
        copies[("CP", q, start)] = ("yp", size)
        copies[("CM", q, start)] = ("ym", size)
        steps[("XC", q, start)] = (
            2,
            [("x2", u) for u in parts],
            [("FW", *p) for p in pieces],
            0.05,
            [("CP", q, start), ("CM", q, start)],
        )
        copies[("X2", q, start)] = ("x2", size)
        steps[("XX", q, start)] = (1, [("F", q, start)], [], 0.05, [("X2", q, start)])
    for q in range(2):
        whole = cover(q, 0, HALF)
        half = [(q, start) for start in range(0, HALF, piece)]
        arrivals = {
            "00": [],
            "30": [("yp", u) for u in whole],
            "10": [("ym", u) for u in whole],
            "01": [("x2", u) for u in whole],
            "20": [("F", *p) for p in half],
            "31": [("CP", *p) for p in half],
            "11": [("CM", *p) for p in half],
            "21": [("X2", *p) for p in half],
        }
        for slot, needed in arrivals.items():
            before = [("A3", u) for u in whole] if slot == "00" else []
            share = ("S", slot, q)
            copies[share] = ("core", HALF * HALF * 4)
            steps[("SH", slot, q)] = (3, needed, before, 0.05, [share])
            if split:
                steps[("G0", slot, q)] = (5, needed, before, 0.7, [])
                steps[("G1", slot, q)] = (5, [share], [("SH", slot, q)], 0.7, [])
            else:
                steps[("G", slot, q)] = (5, [share], [("SH", slot, q)], 1.31, [])

    free, arrival, done, order = {}, {}, {}, []

    def issue(copy, now):
        flow, size = copies[copy]
        link = "xi" if flow == "x2" else flow
        wire = size / core_rate if flow == "core" else 2 * size / link_rate
        latency = {"core": on_chip, "x2": two_hops}.get(flow, hop)
        free[link] = max(now, free.get(link, 0.0)) + wire
        arrival[copy] = free[link] + latency

    now = 1.0
    for u in range(len(units)):
        issue(("L1", u), now)
    while len(order) < len(steps):
        best = None
        for name, (rank, needed, before, length, sends) in steps.items():
            if name in done or any(b not in done for b in before) or any(n not in arrival for n in needed):
                continue
            ready = max([arrival[n] for n in needed] + [done[b] for b in before] + [0.0])
            if rank == 5:
                ready = max(ready, first_product)
            key = (max(ready, now), rank if ready <= now else 9, ready)
            if best is None or key < best[0]:
                best = (key, name, ready)
        name = best[1]
        now = max(now, best[2]) + steps[name][3]
        done[name] = now
        order.append(name)
        for copy in steps[name][4]:
            issue(copy, now)
    return order, steps, list(copies)


UNITS = units_of(UNIT_ROWS)
ORDER, STEPS, COPIES = plan(UNITS, PIECE, FIRST_PRODUCT, SPLIT_PRODUCT)
COPY_AT = {name: i for i, name in enumerate(COPIES)}


def split_bf16(x):
    high = x.astype(BF16)
    return high, (x - high.astype(F32)).astype(BF16)


def kernel(d_ref, k_ref, o_ref, own, got1, fold1, got2, keep2, give2, got3, gathered, tiles, total, send_sem, recv_sem, own_sem, tile_sem, out_sem):
    c, r = lax.axis_index("irrep"), lax.axis_index("row")
    x_lo, z0, z1 = c % 2, c // 2 % 2, c // 4
    core, x_hi, y = r % 2, r // 2 % 2, r // 4
    to = {
        "xi": (c + 1 - 2 * x_lo, r),
        "zA": (c + 2 - 4 * z0, r),
        "zB": (c + 2 - 4 * z0 + 4 - 8 * z1, r),
        "yp": (c, (r + 4) % 16),
        "ym": (c, (r + 12) % 16),
        "x2": (c, r + 2 - 4 * x_hi),
        "core": (c, r + 1 - 2 * core),
    }
    sign_x = (1 - 2 * x_lo).astype(F32)
    sign_z0 = (1 - 2 * z0).astype(F32)
    sign_z1 = (1 - 2 * z1).astype(F32)
    scale = 1.0 / math.sqrt(8)

    own_copy = pltpu.make_async_copy(d_ref.at[0], own, own_sem)
    own_copy.start()
    barrier = pltpu.get_barrier_semaphore()
    for target in to.values():
        pl.semaphore_signal(barrier, 1, device_id=target, device_id_type=MESH)
    pl.semaphore_wait(barrier, len(to))

    def part(u):
        q, start, count = UNITS[u]
        return pl.ds(start, count), pl.ds(q * HALF, HALF)

    def block(slot, q, start, count, side=0):
        return gathered.at[SLOT[slot], side, pl.ds(start, count), pl.ds(q * HALF, HALF)]

    def describe(name):
        flow = name[0]
        if flow in ("L1", "L2", "L3", "yp", "ym", "x2"):
            u = name[1]
            rows, cols = part(u)
            q, start, count = UNITS[u]
        if flow == "L1":
            source, target, link = d_ref.at[0, rows, cols], got1.at[rows, cols], "xi"
        elif flow == "L2":
            source, target, link = fold1.at[rows, cols], got2.at[rows, cols], "zA"
        elif flow == "L3":
            source, target, link = give2.at[rows, cols], got3.at[rows, cols], "zB"
        elif flow in ("yp", "ym", "x2"):
            slot = {"yp": "30", "ym": "10", "x2": "01"}[flow]
            source, target, link = block("00", q, start, count), block(slot, q, start, count), flow
        elif flow == "S":
            source, target, link = block(name[1], name[2], 0, HALF), block(name[1], name[2], 0, HALF, 1), "core"
        else:
            _, q, start = name
            origin, slot, link = {
                "F": (("10", "30")[q], "20", ("ym", "yp")[q]),
                "CP": ("01", "31", "yp"),
                "CM": ("01", "11", "ym"),
                "X2": ("20", "21", "x2"),
            }[flow]
            source, target = block(origin, q, start, PIECE), block(slot, q, start, PIECE)
        i = COPY_AT[name]
        return pltpu.make_async_remote_copy(
            src_ref=source,
            dst_ref=target,
            send_sem=send_sem.at[i],
            recv_sem=recv_sem.at[i],
            device_id=to[link],
            device_id_type=MESH,
        )

    arrived = set()

    def wait_for(names):
        for name in names:
            if name not in arrived:
                arrived.add(name)
                describe(name).wait_recv()

    for u in range(len(UNITS)):
        describe(("L1", u)).start()
    tile_copies = []
    for i, slot in enumerate(SLOTS):
        block_at = ((y + int(slot[0])) % 4 * 2 + (x_hi + int(slot[1])) % 2) * 2
        for side in range(2):
            owner = block_at + (core + side) % 2
            copy = pltpu.make_async_copy(
                k_ref.at[0, :, pl.ds(pl.multiple_of(owner * HALF, HALF), HALF)],
                tiles.at[2 * i + side],
                tile_sem.at[2 * i + side],
            )
            copy.start()
            tile_copies.append(copy)
    own_copy.wait()

    tiles_in, started = set(), set()

    def product(slot, q, sides):
        left, right = [], []
        for side in sides:
            i = 2 * SLOT[slot] + side
            if i not in tiles_in:
                tiles_in.add(i)
                tile_copies[i].wait()
            high, low = split_bf16(tiles[i])
            b_high, b_low = split_bf16(gathered[SLOT[slot], side, :, q * HALF : (q + 1) * HALF])
            left += [high, low, high]
            right += [b_high, b_high, b_low]
        term = jnp.dot(jnp.concatenate(left, 1), jnp.concatenate(right, 0), preferred_element_type=F32)
        cols = pl.ds(q * HALF, HALF)
        if q in started:
            total[:, cols] += term
        else:
            started.add(q)
            total[:, cols] = term

    left_over = {q: sum(1 for s in STEPS if s[0][0] == "G" and s[2] == q) for q in range(2)}
    out_copies = []
    for name in ORDER:
        kind = name[0]
        _, needed, _, _, sends = STEPS[name]
        wait_for(needed)
        if kind in ("A1", "A2", "A3"):
            rows, cols = part(name[1])
            if kind == "A1":
                fold1[rows, cols] = got1[rows, cols] + sign_x * own[rows, cols]
            elif kind == "A2":
                mine, other = fold1[rows, cols], got2[rows, cols]
                give2[rows, cols] = mine - sign_z0 * other
                keep2[rows, cols] = other + sign_z0 * mine
            else:
                value = (got3[rows, cols] + sign_z1 * keep2[rows, cols]) * scale
                gathered[SLOT["00"], 0, rows, cols] = value
        for copy in sends:
            describe(copy).start()
        if kind[0] == "G":
            slot, q = name[1:]
            product(slot, q, {"G0": (0,), "G1": (1,), "G": (0, 1)}[kind])
            left_over[q] -= 1
            if left_over[q] == 0:
                cols = pl.ds(q * HALF, HALF)
                copy = pltpu.make_async_copy(total.at[:, cols], o_ref.at[0, :, cols], out_sem.at[q])
                copy.start()
                out_copies.append(copy)
    wait_for(COPIES)
    for name in COPIES:
        describe(name).wait_send()
    for copy in out_copies:
        copy.wait()


def body(densities, reduced_kernel):
    rows = reduced_kernel.shape[1]
    stage = pltpu.VMEM((HALF, 2 * HALF), F32)
    return pl.pallas_call(
        kernel,
        out_shape=jax.ShapeDtypeStruct((1, rows, 2 * HALF), F32),
        in_specs=[pl.BlockSpec(memory_space=pl.ANY)] * 2,
        out_specs=pl.BlockSpec(memory_space=pl.ANY),
        scratch_shapes=[stage] * 7
        + [
            pltpu.VMEM((8, 2, HALF, 2 * HALF), F32),
            pltpu.VMEM((16, rows, HALF), F32),
            pltpu.VMEM((rows, 2 * HALF), F32),
            pltpu.SemaphoreType.DMA((len(COPIES),)),
            pltpu.SemaphoreType.DMA((len(COPIES),)),
            pltpu.SemaphoreType.DMA,
            pltpu.SemaphoreType.DMA((16,)),
            pltpu.SemaphoreType.DMA((2,)),
        ],
        compiler_params=pltpu.CompilerParams(
            collective_id=0, has_side_effects=True, vmem_limit_bytes=63 * 2**20
        ),
        name="fold_gather_product",
    )(densities, reduced_kernel)


def solution(mesh):
    placed = (P("irrep", "row", None), P("irrep", "row", None))
    return jax.shard_map(
        body, mesh=mesh, in_specs=placed, out_specs=P("irrep", "row", None), check_vma=False
    )
```

```python
import math

import jax
import jax.numpy as jnp
from jax import lax
from jax.experimental import pallas as pl
from jax.experimental.pallas import tpu as pltpu
from jax.sharding import PartitionSpec as P

F32, BF16 = jnp.float32, jnp.bfloat16
MESH = pl.DeviceIdType.MESH
HALF = 256

SLOTS = ("00", "30", "10", "01", "20", "31", "11", "21")
SLOT = {name: i for i, name in enumerate(SLOTS)}

UNIT_ROWS = ((32,) * 8, (64,) * 4)

RANK = {"A1": 1.3, "A2": 1.6, "A3": -1.8, "FY": 0.2, "FC": 2.5, "XC": 1.1, "SH": 3.9, "G": 6}
FIRST_PRODUCT, FIRST_CROSSED = 0.0, 33.0


def units_of(rows):
    units = []
    for q in range(2):
        start = 0
        for count in rows[q]:
            units.append((q, start, count))
            start += count
    return units


def graph(units):
    steps, copies, landing = {}, {}, {}
    for u, (q, start, count) in enumerate(units):
        along, against = (("YP", "YM"), ("YM", "YP"))[u % 2]
        links = {
            "L1": "xi",
            "L2": "zA",
            "L3": "zB",
            "X": "x2",
            "YP": "yp",
            "YM": "ym",
            "CP": "yp",
            "CM": "ym",
            "FY": along.lower(),
            "FC": "x2",
        }
        for flow, link in links.items():
            copies[(flow, u)] = (link, count * HALF * 4)
        steps[("A1", u)] = ("A1", [("L1", u)], [], 0.15, [("L2", u)])
        steps[("A2", u)] = ("A2", [("L2", u)], [("A1", u)], 0.15, [("L3", u)])
        steps[("A3", u)] = ("A3", [("L3", u)], [("A2", u)], 0.15, [("X", u), ("YP", u), ("YM", u)])
        steps[("FY", u)] = ("FY", [(along, u)], [], 0.05, [("FY", u)])
        steps[("XC", u)] = ("XC", [("X", u)], [], 0.05, [("CP", u), ("CM", u)])
        steps[("FC", u)] = ("FC", [("FY", u)], [], 0.05, [("FC", u)])
        flows = {"00": None, "30": "YP", "10": "YM", "01": "X", "20": "FY", "31": "CP", "11": "CM", "21": "FC"}
        for slot, flow in flows.items():
            arrivals, before = landing.setdefault((slot, q), ([], []))
            if flow is None:
                before.append(("A3", u))
            else:
                arrivals.append((flow, u))
    for (slot, q), (arrivals, before) in landing.items():
        copies[("S", slot, q)] = ("core", HALF * HALF * 4)
        steps[("SH", slot, q)] = ("SH", arrivals, before, 0.05, [("S", slot, q)])
        steps[("G0", slot, q)] = ("G", arrivals, before, 0.85, [])
        steps[("G1", slot, q)] = ("G", [("S", slot, q)], [("SH", slot, q)], 0.85, [])
    return steps, copies


def plan(units, steps, copies):
    latency = {"xi": 1.97, "zA": 1.95, "zB": 3.4, "yp": 3.1, "ym": 3.1, "x2": 4.7, "core": 2.0}
    free, arrival, done, order = {}, {}, {}, []

    def issue(copy, now):
        flow, size = copies[copy]
        link = "xi" if flow == "x2" else flow
        wire = size / 440e3 if flow == "core" else 2 * size / 90.6e3
        free[link] = max(now, free.get(link, 0.0)) + wire
        arrival[copy] = free[link] + latency[flow]

    now = 5.3
    for u in range(len(units)):
        issue(("L1", u), now)
    while len(order) < len(steps):
        best = None
        for name, (kind, needed, before, length, sends) in steps.items():
            if name in done or any(b not in done for b in before) or any(n not in arrival for n in needed):
                continue
            ready = max([arrival[n] for n in needed] + [done[b] for b in before] + [0.0])
            ready = max(ready, {"G": FIRST_PRODUCT, "XC": FIRST_CROSSED}.get(kind, 0.0))
            key = (max(ready, now), RANK[kind] if ready <= now else 9, ready)
            if best is None or key < best[0]:
                best = (key, name, ready)
        name = best[1]
        now = max(now, best[2]) + steps[name][3]
        done[name] = now
        order.append(name)
        for copy in steps[name][4]:
            now += 0.03
            issue(copy, now)
    return order


UNITS = units_of(UNIT_ROWS)
STEPS, COPIES = graph(UNITS)
ORDER = plan(UNITS, STEPS, COPIES)
COPY_AT = {name: i for i, name in enumerate(COPIES)}


def split_bf16(x):
    high = x.astype(BF16)
    return high, (x - high.astype(F32)).astype(BF16)


def kernel(d_ref, k_ref, o_ref, got1, fold1, got2, keep2, give2, got3, gathered, tiles, send_sem, recv_sem, tile_sem):
    c, r = lax.axis_index("irrep"), lax.axis_index("row")
    x_lo, z0, z1 = c % 2, c // 2 % 2, c // 4
    core, x_hi, y = r % 2, r // 2 % 2, r // 4
    to = {
        "xi": (c + 1 - 2 * x_lo, r),
        "zA": (c + 2 - 4 * z0, r),
        "zB": (c + 2 - 4 * z0 + 4 - 8 * z1, r),
        "yp": (c, (r + 4) % 16),
        "ym": (c, (r + 12) % 16),
        "x2": (c, r + 2 - 4 * x_hi),
        "core": (c, r + 1 - 2 * core),
    }
    sign_x = (1 - 2 * x_lo).astype(F32)
    sign_z0 = (1 - 2 * z0).astype(F32)
    sign_z1 = (1 - 2 * z1).astype(F32)
    scale = 1.0 / math.sqrt(8)

    barrier = pltpu.get_barrier_semaphore()
    for target in to.values():
        pl.semaphore_signal(barrier, 1, device_id=target, device_id_type=MESH)
    pl.semaphore_wait(barrier, len(to))

    def part(u):
        q, start, count = UNITS[u]
        return pl.ds(start, count), pl.ds(q * HALF, HALF)

    def block(slot, q, start, count, side=0):
        return gathered.at[SLOT[slot], side, pl.ds(start, count), pl.ds(q * HALF, HALF)]

    def describe(name):
        flow = name[0]
        link = COPIES[name][0]
        if flow == "S":
            source, target = block(name[1], name[2], 0, HALF), block(name[1], name[2], 0, HALF, 1)
        else:
            u = name[1]
            rows, cols = part(u)
            source, target = {
                "L1": lambda: (d_ref.at[0, rows, cols], got1.at[rows, cols]),
                "L2": lambda: (fold1.at[rows, cols], got2.at[rows, cols]),
                "L3": lambda: (give2.at[rows, cols], got3.at[rows, cols]),
                "X": lambda: (block("00", *UNITS[u]), block("01", *UNITS[u])),
                "YP": lambda: (block("00", *UNITS[u]), block("30", *UNITS[u])),
                "YM": lambda: (block("00", *UNITS[u]), block("10", *UNITS[u])),
                "FY": lambda: (block(("30", "10")[u % 2], *UNITS[u]), block("20", *UNITS[u])),
                "CP": lambda: (block("01", *UNITS[u]), block("31", *UNITS[u])),
                "CM": lambda: (block("01", *UNITS[u]), block("11", *UNITS[u])),
                "FC": lambda: (block("20", *UNITS[u]), block("21", *UNITS[u])),
            }[flow]()
        i = COPY_AT[name]
        return pltpu.make_async_remote_copy(
            src_ref=source,
            dst_ref=target,
            send_sem=send_sem.at[i],
            recv_sem=recv_sem.at[i],
            device_id=to[link],
            device_id_type=MESH,
        )

    arrived = set()

    def wait_for(names):
        for name in names:
            if name not in arrived:
                arrived.add(name)
                describe(name).wait_recv()

    for u in range(len(UNITS)):
        describe(("L1", u)).start()
    tile_copies = []
    for i, slot in enumerate(SLOTS):
        block_at = ((y + int(slot[0])) % 4 * 2 + (x_hi + int(slot[1])) % 2) * 2
        for side in range(2):
            owner = block_at + (core + side) % 2
            copy = pltpu.make_async_copy(
                k_ref.at[0, :, pl.ds(pl.multiple_of(owner * HALF, HALF), HALF)],
                tiles.at[2 * i + side],
                tile_sem.at[2 * i + side],
            )
            copy.start()
            tile_copies.append(copy)

    tiles_in = set()

    def run(name):
        kind, needed, _, _, sends = STEPS[name]
        wait_for(needed)
        if kind in ("A1", "A2", "A3"):
            rows, cols = part(name[1])
            if kind == "A1":
                fold1[rows, cols] = got1[rows, cols] + sign_x * d_ref[0, rows, cols]
            elif kind == "A2":
                mine, other = fold1[rows, cols], got2[rows, cols]
                give2[rows, cols] = mine - sign_z0 * other
                keep2[rows, cols] = other + sign_z0 * mine
            else:
                value = (got3[rows, cols] + sign_z1 * keep2[rows, cols]) * scale
                gathered[SLOT["00"], 0, rows, cols] = value
        for copy in sends:
            describe(copy).start()
        if kind == "G":
            i = tile_of(name)
            if i not in tiles_in:
                tiles_in.add(i)
                tile_copies[i].wait()

    def tile_of(name):
        return 2 * SLOT[name[1]] + int(name[0][1])

    products = [name for name in ORDER if name[0][0] == "G"]
    blocks, block_steps = [], []
    for name in ORDER:
        block_steps.append(name)
        if name[0][0] == "G":
            blocks.append(block_steps)
            block_steps = []
    assert not block_steps

    for name in blocks[0]:
        run(name)
    o_ref[...] = jnp.zeros_like(o_ref)

    @pl.loop(0, len(products))
    def _(g):
        def pick(low, high):
            if high - low == 1:
                if low:
                    for name in blocks[low]:
                        run(name)
                name = products[low]
                return jnp.int32(tile_of(name)), jnp.int32(name[2])
            middle = (low + high) // 2
            return lax.cond(g < middle, lambda: pick(low, middle), lambda: pick(middle, high))

        i, q = pick(0, len(products))
        cols = pl.ds(pl.multiple_of(q * HALF, HALF), HALF)
        high, low = split_bf16(tiles[i])
        b_high, b_low = split_bf16(gathered[i // 2, i % 2, :, cols])
        o_ref[0, :, cols] += jnp.dot(
            jnp.concatenate([high, low, high], 1),
            jnp.concatenate([b_high, b_high, b_low], 0),
            preferred_element_type=F32,
        )

    wait_for(COPIES)
    for name in COPIES:
        describe(name).wait_send()


def body(densities, reduced_kernel):
    rows = reduced_kernel.shape[1]
    stage = pltpu.VMEM((HALF, 2 * HALF), F32)
    return pl.pallas_call(
        kernel,
        out_shape=jax.ShapeDtypeStruct((1, rows, 2 * HALF), F32),
        in_specs=[pl.BlockSpec(memory_space=pltpu.VMEM), pl.BlockSpec(memory_space=pl.ANY)],
        out_specs=pl.BlockSpec(memory_space=pltpu.VMEM),
        scratch_shapes=[stage] * 6
        + [
            pltpu.VMEM((8, 2, HALF, 2 * HALF), F32),
            pltpu.VMEM((16, rows, HALF), F32),
            pltpu.SemaphoreType.DMA((len(COPIES),)),
            pltpu.SemaphoreType.DMA((len(COPIES),)),
            pltpu.SemaphoreType.DMA((16,)),
        ],
        compiler_params=pltpu.CompilerParams(
            collective_id=0, has_side_effects=True, vmem_limit_bytes=50 * 2**20
        ),
        name="fold_gather_product",
    )(densities, reduced_kernel)


def solution(mesh):
    placed = (P("irrep", "row", None), P("irrep", "row", None))
    return jax.shard_map(
        body, mesh=mesh, in_specs=placed, out_specs=P("irrep", "row", None), check_vma=False
    )
```

```python
import math

import jax
import jax.numpy as jnp
from jax import lax
from jax.experimental import pallas as pl
from jax.experimental.pallas import tpu as pltpu
from jax.sharding import PartitionSpec as P

F32, BF16 = jnp.float32, jnp.bfloat16
MESH = pl.DeviceIdType.MESH
HALF = 256

SLOTS = ("00", "30", "10", "01", "20", "31", "11", "21")
SLOT = {name: i for i, name in enumerate(SLOTS)}

UNIT_ROWS = ((32,) * 8, (64,) * 4)

RANK = {"A1": 0.88, "A2": 2.27, "A3": 0.54, "FY": 0.3, "FC": 0.5, "XC": 1.75, "XP": 3.92, "XM": 3.92, "SH": 5.32, "G": 6}
FIRST_PRODUCT, FIRST_CROSSED = 0.0, 30.0

OVER_X = (2, 3)


def units_of(rows):
    units = []
    for q in range(2):
        start = 0
        for count in rows[q]:
            units.append((q, start, count))
            start += count
    return units


def graph(units):
    steps, copies, landing = {}, {}, {}
    for u, (q, start, count) in enumerate(units):
        along, against = (("YP", "YM"), ("YM", "YP"))[u % 2]
        links = {
            "L1": "xi",
            "L2": "zA",
            "L3": "zB",
            "X": "x2",
            "YP": "yp",
            "YM": "ym",
            "CP": "x2" if u in OVER_X else "yp",
            "CM": "x2" if u in OVER_X else "ym",
            "FY": along.lower(),
            "FC": "x2",
        }
        for flow, link in links.items():
            copies[(flow, u)] = (link, count * HALF * 4)
        steps[("A1", u)] = ("A1", [("L1", u)], [], 0.15, [("L2", u)])
        steps[("A2", u)] = ("A2", [("L2", u)], [("A1", u)], 0.15, [("L3", u)])
        steps[("A3", u)] = ("A3", [("L3", u)], [("A2", u)], 0.15, [("X", u), ("YP", u), ("YM", u)])
        steps[("FY", u)] = ("FY", [(along, u)], [], 0.05, [("FY", u)])
        if u in OVER_X:
            steps[("XP", u)] = ("XP", [("YP", u)], [], 0.05, [("CP", u)])
            steps[("XM", u)] = ("XM", [("YM", u)], [], 0.05, [("CM", u)])
        else:
            steps[("XC", u)] = ("XC", [("X", u)], [], 0.05, [("CP", u), ("CM", u)])
        steps[("FC", u)] = ("FC", [("FY", u)], [], 0.05, [("FC", u)])
        flows = {"00": None, "30": "YP", "10": "YM", "01": "X", "20": "FY", "31": "CP", "11": "CM", "21": "FC"}
        for slot, flow in flows.items():
            arrivals, before = landing.setdefault((slot, q), ([], []))
            if flow is None:
                before.append(("A3", u))
            else:
                arrivals.append((flow, u))
    for (slot, q), (arrivals, before) in landing.items():
        copies[("S", slot, q)] = ("core", HALF * HALF * 4)
        steps[("SH", slot, q)] = ("SH", arrivals, before, 0.05, [("S", slot, q)])
        steps[("G", slot, q)] = ("G", [("S", slot, q)], [("SH", slot, q)], 1.4, [])
    return steps, copies


def plan(units, steps, copies):
    latency = {"xi": 1.97, "zA": 1.95, "zB": 3.4, "yp": 3.1, "ym": 3.1, "x2": 4.7, "core": 2.0}
    free, arrival, done, order = {}, {}, {}, []

    def issue(copy, now):
        flow, size = copies[copy]
        link = "xi" if flow == "x2" else flow
        wire = size / 440e3 if flow == "core" else 2 * size / 90.6e3
        free[link] = max(now, free.get(link, 0.0)) + wire
        arrival[copy] = free[link] + latency[flow]

    now = 5.3
    for u in range(len(units)):
        issue(("L1", u), now)
    while len(order) < len(steps):
        best = None
        for name, (kind, needed, before, length, sends) in steps.items():
            if name in done or any(b not in done for b in before) or any(n not in arrival for n in needed):
                continue
            ready = max([arrival[n] for n in needed] + [done[b] for b in before] + [0.0])
            ready = max(ready, {"G": FIRST_PRODUCT, "XC": FIRST_CROSSED}.get(kind, 0.0))
            key = (max(ready, now), RANK[kind] if ready <= now else 9, ready)
            if best is None or key < best[0]:
                best = (key, name, ready)
        name = best[1]
        now = max(now, best[2]) + steps[name][3]
        done[name] = now
        order.append(name)
        for copy in steps[name][4]:
            now += 0.03
            issue(copy, now)
    return order


UNITS = units_of(UNIT_ROWS)
STEPS, COPIES = graph(UNITS)
ORDER = plan(UNITS, STEPS, COPIES)
COPY_AT = {name: i for i, name in enumerate(COPIES)}


def split_bf16(x):
    high = x.astype(BF16)
    return high, (x - high.astype(F32)).astype(BF16)


def kernel(d_ref, k_ref, o_ref, got1, fold1, got2, keep2, give2, got3, gathered, tiles, send_sem, recv_sem, tile_sem):
    c, r = lax.axis_index("irrep"), lax.axis_index("row")
    x_lo, z0, z1 = c % 2, c // 2 % 2, c // 4
    core, x_hi, y = r % 2, r // 2 % 2, r // 4
    to = {
        "xi": (c + 1 - 2 * x_lo, r),
        "zA": (c + 2 - 4 * z0, r),
        "zB": (c + 2 - 4 * z0 + 4 - 8 * z1, r),
        "yp": (c, (r + 4) % 16),
        "ym": (c, (r + 12) % 16),
        "x2": (c, r + 2 - 4 * x_hi),
        "core": (c, r + 1 - 2 * core),
    }
    sign_x = (1 - 2 * x_lo).astype(F32)
    sign_z0 = (1 - 2 * z0).astype(F32)
    sign_z1 = (1 - 2 * z1).astype(F32)
    scale = 1.0 / math.sqrt(8)

    barrier = pltpu.get_barrier_semaphore()
    for target in to.values():
        pl.semaphore_signal(barrier, 1, device_id=target, device_id_type=MESH)
    pl.semaphore_wait(barrier, len(to))

    def part(u):
        q, start, count = UNITS[u]
        return pl.ds(start, count), pl.ds(q * HALF, HALF)

    def block(slot, q, start, count, side=0):
        return gathered.at[SLOT[slot], side, pl.ds(start, count), pl.ds(q * HALF, HALF)]

    def describe(name):
        flow = name[0]
        link = COPIES[name][0]
        if flow == "S":
            source, target = block(name[1], name[2], 0, HALF), block(name[1], name[2], 0, HALF, 1)
        else:
            u = name[1]
            rows, cols = part(u)
            source, target = {
                "L1": lambda: (d_ref.at[0, rows, cols], got1.at[rows, cols]),
                "L2": lambda: (fold1.at[rows, cols], got2.at[rows, cols]),
                "L3": lambda: (give2.at[rows, cols], got3.at[rows, cols]),
                "X": lambda: (block("00", *UNITS[u]), block("01", *UNITS[u])),
                "YP": lambda: (block("00", *UNITS[u]), block("30", *UNITS[u])),
                "YM": lambda: (block("00", *UNITS[u]), block("10", *UNITS[u])),
                "FY": lambda: (block(("30", "10")[u % 2], *UNITS[u]), block("20", *UNITS[u])),
                "CP": lambda: (block("30" if u in OVER_X else "01", *UNITS[u]), block("31", *UNITS[u])),
                "CM": lambda: (block("10" if u in OVER_X else "01", *UNITS[u]), block("11", *UNITS[u])),
                "FC": lambda: (block("20", *UNITS[u]), block("21", *UNITS[u])),
            }[flow]()
        i = COPY_AT[name]
        return pltpu.make_async_remote_copy(
            src_ref=source,
            dst_ref=target,
            send_sem=send_sem.at[i],
            recv_sem=recv_sem.at[i],
            device_id=to[link],
            device_id_type=MESH,
        )

    arrived, sent = set(), set()

    def wait_for(names):
        for name in names:
            if name not in arrived:
                arrived.add(name)
                describe(name).wait_recv()

    def wait_sent(names):
        for name in names:
            if name not in sent:
                sent.add(name)
                describe(name).wait_send()

    for u in range(len(UNITS)):
        describe(("L1", u)).start()
    tile_copies = []
    for i, slot in enumerate(SLOTS):
        block_at = ((y + int(slot[0])) % 4 * 2 + (x_hi + int(slot[1])) % 2) * 2
        for side in range(2):
            owner = block_at + (core + side) % 2
            copy = pltpu.make_async_copy(
                k_ref.at[0, :, pl.ds(pl.multiple_of(owner * HALF, HALF), HALF)],
                tiles.at[2 * i + side],
                tile_sem.at[2 * i + side],
            )
            copy.start()
            tile_copies.append(copy)

    tiles_in = set()

    def run(name):
        kind, needed, _, _, sends = STEPS[name]
        wait_for(needed)
        if kind in ("A1", "A2", "A3"):
            rows, cols = part(name[1])
            if kind == "A1":
                fold1[rows, cols] = got1[rows, cols] + sign_x * d_ref[0, rows, cols]
            elif kind == "A2":
                mine, other = fold1[rows, cols], got2[rows, cols]
                give2[rows, cols] = mine - sign_z0 * other
                keep2[rows, cols] = other + sign_z0 * mine
            else:
                value = (got3[rows, cols] + sign_z1 * keep2[rows, cols]) * scale
                gathered[SLOT["00"], 0, rows, cols] = value
        for copy in sends:
            describe(copy).start()
        if kind == "A3":
            wait_sent([("L1", name[1]), ("L2", name[1])])
        if kind == "G":
            i = SLOT[name[1]]
            if i not in tiles_in:
                tiles_in.add(i)
                tile_copies[2 * i].wait()
                tile_copies[2 * i + 1].wait()

    products = [name for name in ORDER if name[0][0] == "G"]
    blocks, block_steps = [], []
    for name in ORDER:
        block_steps.append(name)
        if name[0][0] == "G":
            blocks.append(block_steps)
            block_steps = []
    assert not block_steps

    o_ref[...] = jnp.zeros_like(o_ref)
    for name in blocks[0]:
        run(name)

    @pl.loop(0, len(products))
    def _(g):
        def pick(low, high):
            if high - low == 1:
                if low:
                    for name in blocks[low]:
                        run(name)
                name = products[low]
                return jnp.int32(SLOT[name[1]]), jnp.int32(name[2])
            middle = (low + high) // 2
            return lax.cond(g < middle, lambda: pick(low, middle), lambda: pick(middle, high))

        i, q = pick(0, len(products))
        cols = pl.ds(pl.multiple_of(q * HALF, HALF), HALF)
        left, right = [], []
        for side in range(2):
            high, low = split_bf16(tiles[2 * i + side])
            b_high, b_low = split_bf16(gathered[i, side, :, cols])
            left += [high, low, high]
            right += [b_high, b_high, b_low]
        o_ref[0, :, cols] += jnp.dot(
            jnp.concatenate(left, 1), jnp.concatenate(right, 0), preferred_element_type=F32
        )

    wait_for(COPIES)
    wait_sent(COPIES)


def body(densities, reduced_kernel):
    rows = reduced_kernel.shape[1]
    stage = pltpu.VMEM((HALF, 2 * HALF), F32)
    return pl.pallas_call(
        kernel,
        out_shape=jax.ShapeDtypeStruct((1, rows, 2 * HALF), F32),
        in_specs=[pl.BlockSpec(memory_space=pltpu.VMEM), pl.BlockSpec(memory_space=pl.ANY)],
        out_specs=pl.BlockSpec(memory_space=pltpu.VMEM),
        scratch_shapes=[stage] * 6
        + [
            pltpu.VMEM((8, 2, HALF, 2 * HALF), F32),
            pltpu.VMEM((16, rows, HALF), F32),
            pltpu.SemaphoreType.DMA((len(COPIES),)),
            pltpu.SemaphoreType.DMA((len(COPIES),)),
            pltpu.SemaphoreType.DMA((16,)),
        ],
        compiler_params=pltpu.CompilerParams(
            collective_id=0, has_side_effects=True, vmem_limit_bytes=50 * 2**20
        ),
        name="fold_gather_product",
    )(densities, reduced_kernel)


def solution(mesh):
    placed = (P("irrep", "row", None), P("irrep", "row", None))
    return jax.shard_map(
        body, mesh=mesh, in_specs=placed, out_specs=P("irrep", "row", None), check_vma=False
    )
```

```python
import math

import jax
import jax.numpy as jnp
from jax import lax
from jax.experimental import pallas as pl
from jax.experimental.pallas import tpu as pltpu
from jax.sharding import PartitionSpec as P

F32, BF16 = jnp.float32, jnp.bfloat16
MESH = pl.DeviceIdType.MESH
HALF = 256

SLOTS = ("00", "30", "10", "01", "20", "31", "11", "21")
SLOT = {name: i for i, name in enumerate(SLOTS)}

UNIT_ROWS = ((32,) * 8, (64,) * 4)

RANK = {"A1": 0.19, "A2": 2.02, "A3": -0.64, "FY": 3.74, "FC": 2.59, "XC": 4.73, "XP": 0.52, "XM": 0.52, "SH": 4.19, "G": 6}
FIRST_PRODUCT, FIRST_CROSSED = 26.0, 28.0

OVER_X = (2, 3, 6)


def units_of(rows):
    units = []
    for q in range(2):
        start = 0
        for count in rows[q]:
            units.append((q, start, count))
            start += count
    return units


def graph(units):
    steps, copies, landing = {}, {}, {}
    for u, (q, start, count) in enumerate(units):
        along, against = (("YP", "YM"), ("YM", "YP"))[u % 2]
        links = {
            "L1": "xi",
            "L2": "zA",
            "L3": "zB",
            "X": "x2",
            "YP": "yp",
            "YM": "ym",
            "CP": "x2" if u in OVER_X else "yp",
            "CM": "x2" if u in OVER_X else "ym",
            "FY": along.lower(),
            "FC": "x2",
        }
        for flow, link in links.items():
            copies[(flow, u)] = (link, count * HALF * 4)
        steps[("A1", u)] = ("A1", [("L1", u)], [], 0.15, [("L2", u)])
        steps[("A2", u)] = ("A2", [("L2", u)], [("A1", u)], 0.15, [("L3", u)])
        steps[("A3", u)] = ("A3", [("L3", u)], [("A2", u)], 0.15, [("X", u), ("YP", u), ("YM", u)])
        steps[("FY", u)] = ("FY", [(along, u)], [], 0.05, [("FY", u)])
        if u in OVER_X:
            steps[("XP", u)] = ("XP", [("YP", u)], [], 0.05, [("CP", u)])
            steps[("XM", u)] = ("XM", [("YM", u)], [], 0.05, [("CM", u)])
        else:
            steps[("XC", u)] = ("XC", [("X", u)], [], 0.05, [("CP", u), ("CM", u)])
        steps[("FC", u)] = ("FC", [("FY", u)], [], 0.05, [("FC", u)])
        flows = {"00": None, "30": "YP", "10": "YM", "01": "X", "20": "FY", "31": "CP", "11": "CM", "21": "FC"}
        for slot, flow in flows.items():
            arrivals, before = landing.setdefault((slot, q), ([], []))
            if flow is None:
                before.append(("A3", u))
            else:
                arrivals.append((flow, u))
    for (slot, q), (arrivals, before) in landing.items():
        copies[("S", slot, q)] = ("core", HALF * HALF * 4)
        steps[("SH", slot, q)] = ("SH", arrivals, before, 0.05, [("S", slot, q)])
        steps[("G", slot, q)] = ("G", [("S", slot, q)], [("SH", slot, q)], 1.55, [])
    return steps, copies


def plan(units, steps, copies):
    latency = {"xi": 1.97, "zA": 1.95, "zB": 3.4, "yp": 3.1, "ym": 3.1, "x2": 4.7, "core": 2.0}
    free, arrival, done, order = {}, {}, {}, []

    def issue(copy, now):
        flow, size = copies[copy]
        link = "xi" if flow == "x2" else flow
        wire = size / 440e3 if flow == "core" else 2 * size / 90.6e3
        free[link] = max(now, free.get(link, 0.0)) + wire
        arrival[copy] = free[link] + latency[flow]

    now = 5.3
    for u in range(len(units)):
        issue(("L1", u), now)
    while len(order) < len(steps):
        best = None
        for name, (kind, needed, before, length, sends) in steps.items():
            if name in done or any(b not in done for b in before) or any(n not in arrival for n in needed):
                continue
            ready = max([arrival[n] for n in needed] + [done[b] for b in before] + [0.0])
            ready = max(ready, {"G": FIRST_PRODUCT, "XC": FIRST_CROSSED}.get(kind, 0.0))
            key = (max(ready, now), RANK[kind] if ready <= now else 9, ready)
            if best is None or key < best[0]:
                best = (key, name, ready)
        name = best[1]
        now = max(now, best[2]) + steps[name][3]
        done[name] = now
        order.append(name)
        for copy in steps[name][4]:
            now += 0.03
            issue(copy, now)
    return order


UNITS = units_of(UNIT_ROWS)
STEPS, COPIES = graph(UNITS)
ORDER = plan(UNITS, STEPS, COPIES)
COPY_AT = {name: i for i, name in enumerate(COPIES)}


def split_bf16(x):
    high = x.astype(BF16)
    return high, (x - high.astype(F32)).astype(BF16)


def kernel(d_ref, k_ref, o_ref, got1, fold1, got2, keep2, give2, got3, gathered, tiles, send_sem, recv_sem, tile_sem):
    c, r = lax.axis_index("irrep"), lax.axis_index("row")
    x_lo, z0, z1 = c % 2, c // 2 % 2, c // 4
    core, x_hi, y = r % 2, r // 2 % 2, r // 4
    to = {
        "xi": (c + 1 - 2 * x_lo, r),
        "zA": (c + 2 - 4 * z0, r),
        "zB": (c + 2 - 4 * z0 + 4 - 8 * z1, r),
        "yp": (c, (r + 4) % 16),
        "ym": (c, (r + 12) % 16),
        "x2": (c, r + 2 - 4 * x_hi),
        "core": (c, r + 1 - 2 * core),
    }
    sign_x = (1 - 2 * x_lo).astype(F32)
    sign_z0 = (1 - 2 * z0).astype(F32)
    sign_z1 = (1 - 2 * z1).astype(F32)
    scale = 1.0 / math.sqrt(8)

    barrier = pltpu.get_barrier_semaphore()
    for target in to.values():
        pl.semaphore_signal(barrier, 1, device_id=target, device_id_type=MESH)
    pl.semaphore_wait(barrier, len(to))

    def part(u):
        q, start, count = UNITS[u]
        return pl.ds(start, count), pl.ds(q * HALF, HALF)

    def block(slot, q, start, count, side=0):
        return gathered.at[SLOT[slot], side, pl.ds(start, count), pl.ds(q * HALF, HALF)]

    def describe(name):
        flow = name[0]
        link = COPIES[name][0]
        if flow == "S":
            source, target = block(name[1], name[2], 0, HALF), block(name[1], name[2], 0, HALF, 1)
        else:
            u = name[1]
            rows, cols = part(u)
            source, target = {
                "L1": lambda: (d_ref.at[0, rows, cols], got1.at[rows, cols]),
                "L2": lambda: (fold1.at[rows, cols], got2.at[rows, cols]),
                "L3": lambda: (give2.at[rows, cols], got3.at[rows, cols]),
                "X": lambda: (block("00", *UNITS[u]), block("01", *UNITS[u])),
                "YP": lambda: (block("00", *UNITS[u]), block("30", *UNITS[u])),
                "YM": lambda: (block("00", *UNITS[u]), block("10", *UNITS[u])),
                "FY": lambda: (block(("30", "10")[u % 2], *UNITS[u]), block("20", *UNITS[u])),
                "CP": lambda: (block("30" if u in OVER_X else "01", *UNITS[u]), block("31", *UNITS[u])),
                "CM": lambda: (block("10" if u in OVER_X else "01", *UNITS[u]), block("11", *UNITS[u])),
                "FC": lambda: (block("20", *UNITS[u]), block("21", *UNITS[u])),
            }[flow]()
        i = COPY_AT[name]
        return pltpu.make_async_remote_copy(
            src_ref=source,
            dst_ref=target,
            send_sem=send_sem.at[i],
            recv_sem=recv_sem.at[i],
            device_id=to[link],
            device_id_type=MESH,
        )

    arrived, sent = set(), set()

    def wait_for(names):
        for name in names:
            if name not in arrived:
                arrived.add(name)
                describe(name).wait_recv()

    def wait_sent(names):
        for name in names:
            if name not in sent:
                sent.add(name)
                describe(name).wait_send()

    for u in range(len(UNITS)):
        describe(("L1", u)).start()
    tile_copies = []
    for i, slot in enumerate(SLOTS):
        block_at = ((y + int(slot[0])) % 4 * 2 + (x_hi + int(slot[1])) % 2) * 2
        for side in range(2):
            owner = block_at + (core + side) % 2
            copy = pltpu.make_async_copy(
                k_ref.at[0, :, pl.ds(pl.multiple_of(owner * HALF, HALF), HALF)],
                tiles.at[2 * i + side],
                tile_sem.at[2 * i + side],
            )
            copy.start()
            tile_copies.append(copy)

    tiles_in = set()

    def run(name):
        kind, needed, _, _, sends = STEPS[name]
        wait_for(needed)
        if kind in ("A1", "A2", "A3"):
            rows, cols = part(name[1])
            if kind == "A1":
                fold1[rows, cols] = got1[rows, cols] + sign_x * d_ref[0, rows, cols]
            elif kind == "A2":
                mine, other = fold1[rows, cols], got2[rows, cols]
                give2[rows, cols] = mine - sign_z0 * other
                keep2[rows, cols] = other + sign_z0 * mine
            else:
                value = (got3[rows, cols] + sign_z1 * keep2[rows, cols]) * scale
                gathered[SLOT["00"], 0, rows, cols] = value
        for copy in sends:
            describe(copy).start()
        if kind == "A3":
            wait_sent([("L1", name[1]), ("L2", name[1])])
        if kind == "G":
            i = SLOT[name[1]]
            if i not in tiles_in:
                tiles_in.add(i)
                tile_copies[2 * i].wait()
                tile_copies[2 * i + 1].wait()

    products = [name for name in ORDER if name[0][0] == "G"]
    blocks, block_steps = [], []
    for name in ORDER:
        block_steps.append(name)
        if name[0][0] == "G":
            blocks.append(block_steps)
            block_steps = []
    assert not block_steps

    o_ref[...] = jnp.zeros_like(o_ref)
    for name in blocks[0]:
        run(name)

    @pl.loop(0, len(products))
    def _(g):
        def pick(low, high):
            if high - low == 1:
                if low:
                    for name in blocks[low]:
                        run(name)
                name = products[low]
                return jnp.int32(SLOT[name[1]]), jnp.int32(name[2])
            middle = (low + high) // 2
            return lax.cond(g < middle, lambda: pick(low, middle), lambda: pick(middle, high))

        i, q = pick(0, len(products))
        cols = pl.ds(pl.multiple_of(q * HALF, HALF), HALF)
        left, right = [], []
        for side in range(2):
            high, low = split_bf16(tiles[2 * i + side])
            b_high, b_low = split_bf16(gathered[i, side, :, cols])
            left += [high, low, high]
            right += [b_high, b_high, b_low]
        o_ref[0, :, cols] += jnp.dot(
            jnp.concatenate(left, 1), jnp.concatenate(right, 0), preferred_element_type=F32
        )

    wait_for(COPIES)
    wait_sent(COPIES)


def body(densities, reduced_kernel):
    rows = reduced_kernel.shape[1]
    stage = pltpu.VMEM((HALF, 2 * HALF), F32)
    return pl.pallas_call(
        kernel,
        out_shape=jax.ShapeDtypeStruct((1, rows, 2 * HALF), F32),
        in_specs=[pl.BlockSpec(memory_space=pltpu.VMEM), pl.BlockSpec(memory_space=pl.ANY)],
        out_specs=pl.BlockSpec(memory_space=pltpu.VMEM),
        scratch_shapes=[stage] * 6
        + [
            pltpu.VMEM((8, 2, HALF, 2 * HALF), F32),
            pltpu.VMEM((16, rows, HALF), F32),
            pltpu.SemaphoreType.DMA((len(COPIES),)),
            pltpu.SemaphoreType.DMA((len(COPIES),)),
            pltpu.SemaphoreType.DMA((16,)),
        ],
        compiler_params=pltpu.CompilerParams(
            collective_id=0, has_side_effects=True, vmem_limit_bytes=50 * 2**20
        ),
        name="fold_gather_product",
    )(densities, reduced_kernel)


def solution(mesh):
    placed = (P("irrep", "row", None), P("irrep", "row", None))
    return jax.shard_map(
        body, mesh=mesh, in_specs=placed, out_specs=P("irrep", "row", None), check_vma=False
    )
```

```python
import math

import jax
import jax.numpy as jnp
from jax import lax
from jax.experimental import pallas as pl
from jax.experimental.pallas import tpu as pltpu
from jax.sharding import PartitionSpec as P

F32, BF16 = jnp.float32, jnp.bfloat16
MESH = pl.DeviceIdType.MESH
HALF = 256

SLOTS = ("00", "30", "10", "01", "20", "31", "11", "21")
SLOT = {name: i for i, name in enumerate(SLOTS)}

UNIT_ROWS = ((16, 16, 32, 32, 32, 32, 32, 32, 32), (64,) * 4)

RANK = {"A1": 0.19, "A2": 2.02, "A3": -0.64, "FY": 3.74, "FC": 2.59, "XC": 4.73, "XP": 0.52, "XM": 0.52, "SH": 4.19, "G": 6}
FIRST_PRODUCT, FIRST_CROSSED = 22.0, 28.0

OVER_X = (3, 4, 7)


def units_of(rows):
    units = []
    for q in range(2):
        start = 0
        for count in rows[q]:
            units.append((q, start, count))
            start += count
    return units


def graph(units):
    steps, copies, landing = {}, {}, {}
    for u, (q, start, count) in enumerate(units):
        along, against = (("YP", "YM"), ("YM", "YP"))[u % 2]
        links = {
            "L1": "xi",
            "L2": "zA",
            "L3": "zB",
            "X": "x2",
            "YP": "yp",
            "YM": "ym",
            "CP": "x2" if u in OVER_X else "yp",
            "CM": "x2" if u in OVER_X else "ym",
            "FY": along.lower(),
            "FC": "x2",
        }
        for flow, link in links.items():
            copies[(flow, u)] = (link, count * HALF * 4)
        steps[("A1", u)] = ("A1", [("L1", u)], [], 0.15, [("L2", u)])
        steps[("A2", u)] = ("A2", [("L2", u)], [("A1", u)], 0.15, [("L3", u)])
        steps[("A3", u)] = ("A3", [("L3", u)], [("A2", u)], 0.15, [("X", u), ("YP", u), ("YM", u)])
        steps[("FY", u)] = ("FY", [(along, u)], [], 0.05, [("FY", u)])
        if u in OVER_X:
            steps[("XP", u)] = ("XP", [("YP", u)], [], 0.05, [("CP", u)])
            steps[("XM", u)] = ("XM", [("YM", u)], [], 0.05, [("CM", u)])
        else:
            steps[("XC", u)] = ("XC", [("X", u)], [], 0.05, [("CP", u), ("CM", u)])
        steps[("FC", u)] = ("FC", [("FY", u)], [], 0.05, [("FC", u)])
        flows = {"00": None, "30": "YP", "10": "YM", "01": "X", "20": "FY", "31": "CP", "11": "CM", "21": "FC"}
        for slot, flow in flows.items():
            arrivals, before = landing.setdefault((slot, q), ([], []))
            if flow is None:
                before.append(("A3", u))
            else:
                arrivals.append((flow, u))
    for (slot, q), (arrivals, before) in landing.items():
        copies[("S", slot, q)] = ("core", HALF * HALF * 4)
        steps[("SH", slot, q)] = ("SH", arrivals, before, 0.05, [("S", slot, q)])
        steps[("G", slot, q)] = ("G", [("S", slot, q)], [("SH", slot, q)], 1.55, [])
    return steps, copies


def plan(units, steps, copies):
    latency = {"xi": 1.97, "zA": 1.95, "zB": 3.4, "yp": 3.1, "ym": 3.1, "x2": 4.7, "core": 2.0}
    free, arrival, done, order = {}, {}, {}, []

    def issue(copy, now):
        flow, size = copies[copy]
        link = "xi" if flow == "x2" else flow
        wire = size / 440e3 if flow == "core" else 2 * size / 90.6e3
        free[link] = max(now, free.get(link, 0.0)) + wire
        arrival[copy] = free[link] + latency[flow]

    now = 5.3
    for u in range(len(units)):
        issue(("L1", u), now)
    while len(order) < len(steps):
        best = None
        for name, (kind, needed, before, length, sends) in steps.items():
            if name in done or any(b not in done for b in before) or any(n not in arrival for n in needed):
                continue
            ready = max([arrival[n] for n in needed] + [done[b] for b in before] + [0.0])
            ready = max(ready, {"G": FIRST_PRODUCT, "XC": FIRST_CROSSED}.get(kind, 0.0))
            key = (max(ready, now), RANK[kind] if ready <= now else 9, ready)
            if best is None or key < best[0]:
                best = (key, name, ready)
        name = best[1]
        now = max(now, best[2]) + steps[name][3]
        done[name] = now
        order.append(name)
        for copy in steps[name][4]:
            now += 0.03
            issue(copy, now)
    return order


UNITS = units_of(UNIT_ROWS)
STEPS, COPIES = graph(UNITS)
ORDER = plan(UNITS, STEPS, COPIES)
COPY_AT = {name: i for i, name in enumerate(COPIES)}


def split_bf16(x):
    high = x.astype(BF16)
    return high, (x - high.astype(F32)).astype(BF16)


def kernel(d_ref, k_ref, o_ref, got1, fold1, got2, keep2, give2, got3, gathered, tiles, send_sem, recv_sem, tile_sem):
    c, r = lax.axis_index("irrep"), lax.axis_index("row")
    x_lo, z0, z1 = c % 2, c // 2 % 2, c // 4
    core, x_hi, y = r % 2, r // 2 % 2, r // 4
    to = {
        "xi": (c + 1 - 2 * x_lo, r),
        "zA": (c + 2 - 4 * z0, r),
        "zB": (c + 2 - 4 * z0 + 4 - 8 * z1, r),
        "yp": (c, (r + 4) % 16),
        "ym": (c, (r + 12) % 16),
        "x2": (c, r + 2 - 4 * x_hi),
        "core": (c, r + 1 - 2 * core),
    }
    sign_x = (1 - 2 * x_lo).astype(F32)
    sign_z0 = (1 - 2 * z0).astype(F32)
    sign_z1 = (1 - 2 * z1).astype(F32)
    scale = 1.0 / math.sqrt(8)

    barrier = pltpu.get_barrier_semaphore()
    for target in to.values():
        pl.semaphore_signal(barrier, 1, device_id=target, device_id_type=MESH)
    pl.semaphore_wait(barrier, len(to))

    def part(u):
        q, start, count = UNITS[u]
        return pl.ds(start, count), pl.ds(q * HALF, HALF)

    def block(slot, q, start, count, side=0):
        return gathered.at[SLOT[slot], side, pl.ds(start, count), pl.ds(q * HALF, HALF)]

    def describe(name):
        flow = name[0]
        link = COPIES[name][0]
        if flow == "S":
            source, target = block(name[1], name[2], 0, HALF), block(name[1], name[2], 0, HALF, 1)
        else:
            u = name[1]
            rows, cols = part(u)
            source, target = {
                "L1": lambda: (d_ref.at[0, rows, cols], got1.at[rows, cols]),
                "L2": lambda: (fold1.at[rows, cols], got2.at[rows, cols]),
                "L3": lambda: (give2.at[rows, cols], got3.at[rows, cols]),
                "X": lambda: (block("00", *UNITS[u]), block("01", *UNITS[u])),
                "YP": lambda: (block("00", *UNITS[u]), block("30", *UNITS[u])),
                "YM": lambda: (block("00", *UNITS[u]), block("10", *UNITS[u])),
                "FY": lambda: (block(("30", "10")[u % 2], *UNITS[u]), block("20", *UNITS[u])),
                "CP": lambda: (block("30" if u in OVER_X else "01", *UNITS[u]), block("31", *UNITS[u])),
                "CM": lambda: (block("10" if u in OVER_X else "01", *UNITS[u]), block("11", *UNITS[u])),
                "FC": lambda: (block("20", *UNITS[u]), block("21", *UNITS[u])),
            }[flow]()
        i = COPY_AT[name]
        return pltpu.make_async_remote_copy(
            src_ref=source,
            dst_ref=target,
            send_sem=send_sem.at[i],
            recv_sem=recv_sem.at[i],
            device_id=to[link],
            device_id_type=MESH,
        )

    arrived, sent = set(), set()

    def wait_for(names):
        for name in names:
            if name not in arrived:
                arrived.add(name)
                describe(name).wait_recv()

    def wait_sent(names):
        for name in names:
            if name not in sent:
                sent.add(name)
                describe(name).wait_send()

    for u in range(len(UNITS)):
        describe(("L1", u)).start()
    tile_copies = []
    for i, slot in enumerate(SLOTS):
        block_at = ((y + int(slot[0])) % 4 * 2 + (x_hi + int(slot[1])) % 2) * 2
        for side in range(2):
            owner = block_at + (core + side) % 2
            copy = pltpu.make_async_copy(
                k_ref.at[0, :, pl.ds(pl.multiple_of(owner * HALF, HALF), HALF)],
                tiles.at[2 * i + side],
                tile_sem.at[2 * i + side],
            )
            copy.start()
            tile_copies.append(copy)

    tiles_in = set()

    def run(name):
        kind, needed, _, _, sends = STEPS[name]
        wait_for(needed)
        if kind in ("A1", "A2", "A3"):
            rows, cols = part(name[1])
            if kind == "A1":
                fold1[rows, cols] = got1[rows, cols] + sign_x * d_ref[0, rows, cols]
            elif kind == "A2":
                mine, other = fold1[rows, cols], got2[rows, cols]
                give2[rows, cols] = mine - sign_z0 * other
                keep2[rows, cols] = other + sign_z0 * mine
            else:
                value = (got3[rows, cols] + sign_z1 * keep2[rows, cols]) * scale
                gathered[SLOT["00"], 0, rows, cols] = value
        for copy in sends:
            describe(copy).start()
        if kind == "A3":
            wait_sent([("L1", name[1]), ("L2", name[1])])
        if kind == "G":
            i = SLOT[name[1]]
            if i not in tiles_in:
                tiles_in.add(i)
                tile_copies[2 * i].wait()
                tile_copies[2 * i + 1].wait()

    products = [name for name in ORDER if name[0][0] == "G"]
    blocks, block_steps = [], []
    for name in ORDER:
        block_steps.append(name)
        if name[0][0] == "G":
            blocks.append(block_steps)
            block_steps = []
    assert not block_steps

    o_ref[...] = jnp.zeros_like(o_ref)
    for name in blocks[0]:
        run(name)

    @pl.loop(0, len(products))
    def _(g):
        def pick(low, high):
            if high - low == 1:
                if low:
                    for name in blocks[low]:
                        run(name)
                name = products[low]
                return jnp.int32(SLOT[name[1]]), jnp.int32(name[2])
            middle = (low + high) // 2
            return lax.cond(g < middle, lambda: pick(low, middle), lambda: pick(middle, high))

        i, q = pick(0, len(products))
        cols = pl.ds(pl.multiple_of(q * HALF, HALF), HALF)
        left, right = [], []
        for side in range(2):
            high, low = split_bf16(tiles[2 * i + side])
            b_high, b_low = split_bf16(gathered[i, side, :, cols])
            left += [high, low, high]
            right += [b_high, b_high, b_low]
        o_ref[0, :, cols] += jnp.dot(
            jnp.concatenate(left, 1), jnp.concatenate(right, 0), preferred_element_type=F32
        )

    wait_for(COPIES)
    wait_sent(COPIES)


def body(densities, reduced_kernel):
    rows = reduced_kernel.shape[1]
    stage = pltpu.VMEM((HALF, 2 * HALF), F32)
    return pl.pallas_call(
        kernel,
        out_shape=jax.ShapeDtypeStruct((1, rows, 2 * HALF), F32),
        in_specs=[pl.BlockSpec(memory_space=pltpu.VMEM), pl.BlockSpec(memory_space=pl.ANY)],
        out_specs=pl.BlockSpec(memory_space=pltpu.VMEM),
        scratch_shapes=[stage] * 6
        + [
            pltpu.VMEM((8, 2, HALF, 2 * HALF), F32),
            pltpu.VMEM((16, rows, HALF), F32),
            pltpu.SemaphoreType.DMA((len(COPIES),)),
            pltpu.SemaphoreType.DMA((len(COPIES),)),
            pltpu.SemaphoreType.DMA((16,)),
        ],
        compiler_params=pltpu.CompilerParams(
            collective_id=0, has_side_effects=True, vmem_limit_bytes=50 * 2**20
        ),
        name="fold_gather_product",
    )(densities, reduced_kernel)


def solution(mesh):
    placed = (P("irrep", "row", None), P("irrep", "row", None))
    return jax.shard_map(
        body, mesh=mesh, in_specs=placed, out_specs=P("irrep", "row", None), check_vma=False
    )
```
